32 devices in a mesh: ind: 16 (over z, x, core), snp: 2 (over y).
Axes of the slice: x: 2, y: 2, z: 4, core: 2. Of those that a mesh axis runs over, the one named last changes fastest.
Arguments:
- genotypes: int32 [16384, 512], P('ind', 'snp'), may hold values from 0 to 2
- covariates: float32 [16384, 40], P('ind'), may hold values from -5 to 7
- traits: bfloat16 [16384, 3072], P('ind', 'snp'), may hold values from -17 to 17
Outputs:
- zscores: float32 [512, 3072], P('snp', 'ind')
The draws below stay inside these ranges and needn't reach their ends.
All inputs are finite; a program needn't handle non-finite values.
Results may differ from the reference program's by a relative error of at most 0.0041.
Values may be sent and summed in bfloat16 or wider, within the bound.
A program may use at most 64 MiB of HBM per device.

```python
import jax
import jax.numpy as jnp
from jax import lax

P_SIZE = 3072
K = 40
NIND = 16384
M = 512


def group_signs(key):
    base = jax.random.fold_in(key, 11)
    label = jax.random.randint(jax.random.fold_in(base, 4), (NIND, 1), 0, 2)
    return 2 * label - 1


def dosage_table(key):
    base = jax.random.fold_in(key, 11)
    signs = group_signs(key)
    freq = jax.random.randint(jax.random.fold_in(base, 1), (1, M), 50, 951)
    shift = jax.random.randint(jax.random.fold_in(base, 5), (1, M), -150, 151)
    group_freq = jnp.clip(freq + shift * signs, 50, 950)
    first = jax.random.randint(jax.random.fold_in(base, 2), (NIND, M), 0, 1000)
    second = jax.random.randint(jax.random.fold_in(base, 3), (NIND, M), 0, 1000)
    return (first < group_freq).astype(jnp.int32) + (second < group_freq).astype(jnp.int32)


def covariate_table(key):
    table = dosage_table(key)
    signs = group_signs(key).astype(jnp.float32)
    step_cols = M // K
    linked = table[:, ::step_cols][:, :K].astype(jnp.float32)
    base = jax.random.fold_in(key, 23)
    means = jax.random.uniform(jax.random.fold_in(base, 1), (1, K), jnp.float32, 0.5, 2.0)
    noise = jnp.clip(jax.random.normal(jax.random.fold_in(base, 2), (NIND, K), jnp.float32), -4.0, 4.0)
    linked_part = means + noise + 0.8 * (linked - 1.0)
    ancestry = means[:, :1] + 1.5 * signs + 0.5 * noise[:, :1]
    return jnp.concatenate([ancestry, linked_part[:, 1:]], axis=1)


def draw_genotypes(key, part):
    return dosage_table(key)


def draw_covariates(key, part):
    return covariate_table(key)


def draw_traits(key, part):
    table = covariate_table(key)
    base = jax.random.fold_in(key, 37)
    ramp = 0.5 + 1.5 * jnp.arange(NIND, dtype=jnp.float32)[:, None] / NIND
    noise = jnp.clip(jax.random.normal(jax.random.fold_in(base, 1), (NIND, P_SIZE), jnp.float32), -4.0, 4.0)
    weights = jax.random.uniform(jax.random.fold_in(base, 2), (1, P_SIZE), jnp.float32, 0.3, 0.6)
    columns = jnp.arange(P_SIZE)
    linked = table[:, columns % K] + table[:, (columns + 7) % K]
    return (ramp * noise + weights * linked).astype(jnp.bfloat16)


def setup_inputs(seed: int = 0) -> dict:
    streams_of = jax.random.split(jax.random.key(seed), 4)
    return {
        "genotypes": draw_genotypes(jax.random.fold_in(streams_of[3], 71), 0),
        "covariates": draw_covariates(jax.random.fold_in(streams_of[3], 71), 0),
        "traits": draw_traits(jax.random.fold_in(streams_of[3], 71), 0),
    }


EPS = 1e-05

def reference(genotypes, covariates, traits):
    highest = lax.Precision.HIGHEST
    geno = genotypes.astype(jnp.float32)
    trait_full = traits.astype(jnp.float32)
    cross_cov = jnp.dot(covariates.T, covariates, precision=highest)
    cross_geno = jnp.dot(covariates.T, geno, precision=highest)
    cross_trait = jnp.dot(covariates.T, trait_full, precision=highest)
    factor = jnp.linalg.cholesky(cross_cov)
    coef_geno = jax.scipy.linalg.cho_solve((factor, True), cross_geno)
    coef_trait = jax.scipy.linalg.cho_solve((factor, True), cross_trait)
    geno_res = geno - jnp.dot(covariates, coef_geno, precision=highest)
    trait_res = trait_full - jnp.dot(covariates, coef_trait, precision=highest)
    variance = lax.optimization_barrier(jnp.sum(geno_res * geno_res, axis=0))
    trait_norm = lax.optimization_barrier(jnp.sum(trait_res * trait_res, axis=0))
    geno_low = geno_res.astype(jnp.bfloat16)
    scale = lax.rsqrt(trait_norm / (NIND - K) + EPS)
    trait_low = (trait_res * scale[None, :]).astype(jnp.bfloat16)
    scores = lax.dot_general(geno_low.astype(jnp.float32), trait_low.astype(jnp.float32), (((0,), (0,)), ((), ())), preferred_element_type=jnp.float32)
    return scores * lax.rsqrt(variance + EPS)[:, None]
```

```python
import jax
import jax.numpy as jnp
from jax import lax
from jax.sharding import PartitionSpec as P

K = 40


EPS = 1e-05


def split3(x):
    high = lax.reduce_precision(x, 8, 7)
    rest = x - high
    middle = lax.reduce_precision(rest, 8, 7)
    low = rest - middle
    return [part.astype(jnp.bfloat16) for part in (high, middle, low)]


def per_device(genotypes, covariates, traits):
    highest = lax.Precision.HIGHEST
    n_ind, n_snp = lax.axis_size("ind"), lax.axis_size("snp")
    count = genotypes.shape[0] * n_ind
    k = covariates.shape[1]
    geno = lax.all_gather(genotypes.astype(jnp.bfloat16), "snp", axis=1, tiled=True)
    m = geno.shape[1]
    rows = (((0,), (0,)), ((), ()))
    cov = jnp.concatenate(split3(covariates), axis=1)
    both = jnp.concatenate([geno, cov], axis=1)
    prod = lax.dot_general(traits, both, rows, preferred_element_type=jnp.float32)
    local = traits.astype(jnp.float32)
    squares = jnp.sum(local * local, axis=0)
    sent = jnp.concatenate(
        [
            prod[:, :m],
            prod[:, m : m + k] + prod[:, m + k : m + 2 * k] + prod[:, m + 2 * k :],
            squares[:, None],
        ],
        axis=1,
    )
    gram = lax.dot_general(both, cov, rows, preferred_element_type=jnp.float32)
    gram = gram[:, :k] + gram[:, k : 2 * k] + gram[:, 2 * k :]
    gram_cov = gram[m : m + k] + gram[m + k : m + 2 * k] + gram[m + 2 * k :]
    wide = geno.astype(jnp.float32)
    gram_sq = jnp.sum(wide * wide, axis=0)
    cross_cov, cross_geno, geno_sq = lax.psum((gram_cov, gram[:m], gram_sq), "ind")
    mine = lax.psum_scatter(sent, "ind", scatter_dimension=0, tiled=True)
    unit = mine.shape[0]

    factor = jnp.linalg.cholesky(cross_cov)
    inverse = jax.scipy.linalg.solve_triangular(
        factor, jnp.eye(k, dtype=jnp.float32), lower=True
    )
    geno_w = jnp.dot(cross_geno, inverse.T, precision=highest)
    trait_w = jnp.dot(mine[:, m : m + k], inverse.T, precision=highest)
    variance = geno_sq - jnp.sum(geno_w * geno_w, axis=1)
    trait_norm = mine[:, m + k] - jnp.sum(trait_w * trait_w, axis=1)
    fit = lax.dot_general(trait_w, geno_w, (((1,), (1,)), ((), ())), precision=highest)
    scale = lax.rsqrt(trait_norm / (count - k) + EPS)
    z = (mine[:, :m] - fit) * scale[:, None] * lax.rsqrt(variance + EPS)[None, :]

    me_i, me_s = lax.axis_index("ind"), lax.axis_index("snp")
    blocks = z.reshape(unit, n_snp, m // n_snp)
    place = lax.rem(me_s * n_ind + me_i, n_snp)
    got = jnp.zeros((n_snp, unit, m // n_snp), jnp.float32)
    for step in range(n_snp):
        perm = []
        for i in range(n_ind):
            for s in range(n_snp):
                block = s * n_ind + i
                half = (block % n_snp + step) % n_snp
                perm.append((i * n_snp + s, block // n_snp * n_snp + half))
        out = lax.dynamic_index_in_dim(
            blocks, lax.rem(place + step, n_snp), axis=1, keepdims=False
        )
        arrived = lax.ppermute(out, ("ind", "snp"), perm)
        source = lax.rem(me_s + n_snp - step, n_snp)
        got = lax.dynamic_update_index_in_dim(got, arrived, source, axis=0)
    return got.reshape(n_snp * unit, m // n_snp).T


def solution(mesh):
    in_specs = (P("ind", "snp"), P("ind", None), P("ind", "snp"))
    out_specs = P("snp", "ind")
    return jax.shard_map(
        per_device, mesh=mesh, in_specs=in_specs, out_specs=out_specs, check_vma=False
    )
```

```python
import functools

import jax
import jax.numpy as jnp
from jax import lax
from jax.experimental import pallas as pl
from jax.experimental.pallas import tpu as pltpu
from jax.sharding import PartitionSpec as P

EPS = 1e-05
MESH = pl.DeviceIdType.MESH
LANES = 128


def split3(x):
    high = lax.reduce_precision(x, 8, 7)
    rest = x - high
    middle = lax.reduce_precision(rest, 8, 7)
    low = rest - middle
    return [part.astype(jnp.bfloat16) for part in (high, middle, low)]


def sum_kernel(
    n, per, part, xpart, small, out, xout, sout,
    r0, h0, r1, h1, yb, r2, h2, rf,
    xr0, xh0, xr1, xh1, xyb, xr2, xh2, xrf,
    sbuf, srecv, sfin,
    send0, recv0, send1, recv1, sendy, recvy, send2, recv2, sendf, recvf, ssend, srec,
):
    me = lax.axis_index("ind")
    mine = lax.axis_index("snp")
    bits = [lax.rem(me // (1 << b), 2) for b in range(3)]
    pair = [me + (1 - 2 * bits[b]) * (1 << b) for b in range(3)]
    top = me // 8
    low = lax.rem(me, 8)

    def up(d):
        return lax.rem(top + d, n)

    def side(d):
        return lax.rem(mine + d, n)

    barrier = pltpu.get_barrier_semaphore()
    for b in range(3):
        pl.semaphore_signal(barrier, inc=1, device_id={"ind": pair[b]}, device_id_type=MESH)
    for d in range(1, n):
        pl.semaphore_signal(
            barrier, inc=1, device_id={"ind": low + 8 * up(d)}, device_id_type=MESH
        )
        pl.semaphore_signal(barrier, inc=1, device_id={"snp": side(d)}, device_id_type=MESH)
    pl.semaphore_wait(barrier, 3 + 2 * (n - 1))

    started = []

    def send(src, dst, ssem, rsem, target):
        copy = pltpu.make_async_remote_copy(
            src_ref=src, dst_ref=dst, send_sem=ssem, recv_sem=rsem,
            device_id=target, device_id_type=MESH,
        )
        copy.start()
        started.append(copy)
        return copy

    chunks = [(k, q) for k in range(1, n) for q in range(per)] + [None]
    chunks += [(0, q) for q in range(per)]
    total = len(chunks)
    first, second, third, last, across = {}, {}, {}, {}, {}

    def cols(c):
        k, q = chunks[c]
        return pl.ds((k * per + q) * LANES, LANES)

    def stage0(c):
        if chunks[c] is None:
            src, dst = xpart.at[:, :, 1 - bits[0]], xr0
        else:
            src, dst = part.at[:, :, 1 - bits[0], :, cols(c)], r0.at[c]
        first[c] = send(src, dst, send0.at[c], recv0.at[c], {"ind": pair[0]})

    def stage1(c):
        first[c].wait_recv()
        if chunks[c] is None:
            xh0[...] = xpart[:, :, bits[0]] + xr0[...]
            src, dst = xh0.at[:, 1 - bits[1]], xr1
        else:
            h0[c] = part[:, :, bits[0], :, cols(c)] + r0[c]
            src, dst = h0.at[c, :, 1 - bits[1]], r1.at[c]
        second[c] = send(src, dst, send1.at[c], recv1.at[c], {"ind": pair[1]})

    def stage2(c):
        second[c].wait_recv()
        if chunks[c] is None:
            xyb[mine] = xh0[:, bits[1]] + xr1[...]
            across[c] = [
                send(xyb.at[mine], xyb.at[mine], sendy.at[c, d - 1], recvy.at[c, d - 1], {"snp": side(d)})
                for d in range(1, n)
            ]
        else:
            k, q = chunks[c]
            value = h0[c, :, bits[1]] + r1[c]
            if k == 0:
                yb[q, mine] = value
            else:
                h1[c] = value
                across[k, q] = send(
                    h1.at[c], yb.at[q, mine], sendy.at[c, 0], recvy.at[c, 0], {"snp": side(k)}
                )

    def stage3(c):
        if chunks[c] is None:
            for copy in across[c]:
                copy.wait_recv()
            third[c] = send(
                xyb.at[:, 1 - bits[2]], xr2, send2.at[c], recv2.at[c], {"ind": pair[2]}
            )
        elif chunks[c][0] == 0:
            q = chunks[c][1]
            for k in range(1, n):
                across[k, q].wait_recv()
            third[c] = send(
                yb.at[q, :, 1 - bits[2]], r2.at[q], send2.at[c], recv2.at[c], {"ind": pair[2]}
            )

    def stage4(c):
        if chunks[c] is None:
            third[c].wait_recv()
            xh2[...] = xyb[:, bits[2]] + xr2[...]
            last[c] = [
                send(xh2.at[up(d)], xrf.at[d - 1], sendf.at[c, d - 1], recvf.at[c, d - 1], {"ind": low + 8 * up(d)})
                for d in range(1, n)
            ]
        elif chunks[c][0] == 0:
            q = chunks[c][1]
            third[c].wait_recv()
            h2[q] = yb[q, :, bits[2]] + r2[q]
            last[c] = [
                send(h2.at[q, up(d)], rf.at[q, d - 1], sendf.at[c, d - 1], recvf.at[c, d - 1], {"ind": low + 8 * up(d)})
                for d in range(1, n)
            ]

    def stage5(c):
        if chunks[c] is None:
            value = xh2[top]
            for d in range(1, n):
                last[c][d - 1].wait_recv()
                value = value + xrf[d - 1]
            xout[...] = value
        elif chunks[c][0] == 0:
            q = chunks[c][1]
            value = h2[q, top]
            for d in range(1, n):
                last[c][d - 1].wait_recv()
                value = value + rf[q, d - 1]
            out[:, q * LANES : (q + 1) * LANES] = value

    tiny = {}

    def small_step(b):
        if b > 0:
            tiny[b - 1].wait_recv()
            sbuf[b - 1] = (small[...] if b == 1 else sbuf[b - 2]) + srecv[b - 1]
        if b < 3:
            src = small if b == 0 else sbuf.at[b - 1]
            tiny[b] = send(src, srecv.at[b], ssend.at[b], srec.at[b], {"ind": pair[b]})
        else:
            tiny[3] = [
                send(sbuf.at[2], sfin.at[d - 1], ssend.at[2 + d], srec.at[2 + d], {"ind": low + 8 * up(d)})
                for d in range(1, n)
            ]

    def small_end():
        value = sbuf[2]
        for d in range(1, n):
            tiny[3][d - 1].wait_recv()
            value = value + sfin[d - 1]
        sout[...] = value

    small_step(0)
    for c in range(total):
        stage0(c)
    stages = [stage1, stage2, stage3, stage4, stage5]
    for tick in range(total + len(stages) - 1):
        for index in range(len(stages)):
            c = tick - index
            if 0 <= c < total:
                stages[index](c)
        if tick < 3:
            small_step(tick + 1)
        if tick == 3:
            small_end()
    for copy in started:
        copy.wait_send()


def reduce_all(n, part, xpart, small):
    rows, width = part.shape[3], part.shape[4]
    per = width // n // LANES
    total = n * per + 1
    xrows = xpart.shape[3]
    f32 = jnp.float32
    dma = pltpu.SemaphoreType.DMA
    vmem = pl.BlockSpec(memory_space=pltpu.VMEM)
    peers = max(n - 1, 1)
    return pl.pallas_call(
        functools.partial(sum_kernel, n, per),
        out_shape=[
            jax.ShapeDtypeStruct((rows, per * LANES), f32),
            jax.ShapeDtypeStruct((xrows, LANES), f32),
            jax.ShapeDtypeStruct(small.shape, f32),
        ],
        in_specs=[vmem] * 3,
        out_specs=[vmem] * 3,
        scratch_shapes=[
            pltpu.VMEM((total, 2, 2, rows, LANES), f32),
            pltpu.VMEM((total, 2, 2, rows, LANES), f32),
            pltpu.VMEM((total, 2, rows, LANES), f32),
            pltpu.VMEM((total, 2, rows, LANES), f32),
            pltpu.VMEM((per, n, 2, rows, LANES), f32),
            pltpu.VMEM((per, n, rows, LANES), f32),
            pltpu.VMEM((per, n, rows, LANES), f32),
            pltpu.VMEM((per, peers, rows, LANES), f32),
            pltpu.VMEM((2, 2, xrows, LANES), f32),
            pltpu.VMEM((2, 2, xrows, LANES), f32),
            pltpu.VMEM((2, xrows, LANES), f32),
            pltpu.VMEM((2, xrows, LANES), f32),
            pltpu.VMEM((n, 2, xrows, LANES), f32),
            pltpu.VMEM((n, xrows, LANES), f32),
            pltpu.VMEM((n, xrows, LANES), f32),
            pltpu.VMEM((peers, xrows, LANES), f32),
            pltpu.VMEM((3,) + small.shape, f32),
            pltpu.VMEM((3,) + small.shape, f32),
            pltpu.VMEM((peers,) + small.shape, f32),
            dma((total,)), dma((total,)), dma((total,)), dma((total,)),
            dma((total, peers)), dma((total, peers)),
            dma((total,)), dma((total,)),
            dma((total, peers)), dma((total, peers)),
            dma((3 + peers,)), dma((3 + peers,)),
        ],
        compiler_params=pltpu.CompilerParams(
            collective_id=0, has_side_effects=True, vmem_limit_bytes=40 << 20
        ),
    )(part, xpart, small)


def per_device(genotypes, covariates, traits):
    highest = lax.Precision.HIGHEST
    n_ind, n_snp = lax.axis_size("ind"), lax.axis_size("snp")
    count = genotypes.shape[0] * n_ind
    k = covariates.shape[1]
    m = genotypes.shape[1]
    width = traits.shape[1]
    block = width // 8
    third = block // 3
    assert n_ind == 8 * n_snp and block % 24 == 0 and m % LANES == 0 and k <= 41
    geno = genotypes.astype(jnp.bfloat16)
    shifted = [geno] + [
        lax.ppermute(geno, "snp", [((s + d) % n_snp, s) for s in range(n_snp)])
        for d in range(1, n_snp)
    ]
    rows = (((0,), (0,)), ((), ()))
    cov = jnp.concatenate(split3(covariates), axis=1)

    gram = lax.dot_general(
        cov, jnp.concatenate([geno, cov], axis=1), rows, preferred_element_type=jnp.float32
    )
    gram = gram[:k] + gram[k : 2 * k] + gram[2 * k :]
    gram_cov = gram[:, m : m + k] + gram[:, m + k : m + 2 * k] + gram[:, m + 2 * k :]
    wide = genotypes.astype(jnp.float32)
    squares = jnp.sum(wide * wide, axis=0)
    small = jnp.concatenate([gram[:, :m], squares[None]], axis=0)
    small = jnp.concatenate([small, jnp.pad(gram_cov, ((0, 1), (0, LANES - k)))], axis=1)
    small = jnp.pad(small, ((0, 7 - k % 8), (0, 0)))

    local = traits.astype(jnp.float32)
    xt = lax.dot_general(traits, cov, rows, preferred_element_type=jnp.float32)
    xt = xt[:, :k] + xt[:, k : 2 * k] + xt[:, 2 * k :]
    xt = jnp.concatenate([xt, jnp.sum(local * local, axis=0)[:, None]], axis=1)
    xt = xt.reshape(8, 3, third, k + 1).transpose(0, 2, 1, 3).reshape(8, third, 3 * (k + 1))
    xt = jnp.pad(xt, ((0, 0), (0, 0), (0, LANES - 3 * (k + 1)))).reshape(2, 2, 2, third, LANES)

    both = jnp.concatenate(shifted, axis=1)
    prod = lax.dot_general(traits, both, rows, preferred_element_type=jnp.float32)
    prod = prod.reshape(2, 2, 2, block, n_snp * m)

    mine, xmine, sums = reduce_all(n_snp, prod, xt, small)
    xmine = xmine[:, : 3 * (k + 1)].reshape(third, 3, k + 1).transpose(1, 0, 2).reshape(block, k + 1)

    factor = jnp.linalg.cholesky(sums[:k, m : m + k])
    inverse = jax.scipy.linalg.solve_triangular(
        factor, jnp.eye(k, dtype=jnp.float32), lower=True
    )
    geno_w = jnp.dot(inverse, sums[:k, :m], precision=highest)
    trait_w = jnp.dot(xmine[:, :k], inverse.T, precision=highest)
    variance = sums[k, :m] - jnp.sum(geno_w * geno_w, axis=0)
    trait_norm = xmine[:, k] - jnp.sum(trait_w * trait_w, axis=1)
    fit = jnp.dot(trait_w, geno_w, precision=highest)
    scale = lax.rsqrt(trait_norm / (count - k) + EPS)
    z = (mine - fit) * scale[:, None] * lax.rsqrt(variance + EPS)[None, :]
    return z.T


def solution(mesh):
    in_specs = (P("ind", "snp"), P("ind", None), P("ind", "snp"))
    out_specs = P("snp", "ind")
    return jax.shard_map(
        per_device, mesh=mesh, in_specs=in_specs, out_specs=out_specs, check_vma=False
    )
```

```python
import functools

import jax
import jax.numpy as jnp
from jax import lax
from jax.experimental import pallas as pl
from jax.experimental.pallas import tpu as pltpu
from jax.sharding import PartitionSpec as P

EPS = 1e-05
MESH = pl.DeviceIdType.MESH
LANES = 128


def split3(x):
    high = lax.reduce_precision(x, 8, 7)
    rest = x - high
    middle = lax.reduce_precision(rest, 8, 7)
    low = rest - middle
    return [part.astype(jnp.bfloat16) for part in (high, middle, low)]


def sum_kernel(
    n, per, k_cov, dof, part, xpart, small, out,
    r0, h0, r1, h1, yb, r2, h2, rf,
    xr0, xh0, xr1, xh1, xyb, xr2, xh2, xrf,
    sbuf, srecv, sfin,
    send0, recv0, send1, recv1, sendy, recvy, send2, recv2, sendf, recvf, ssend, srec,
):
    me = lax.axis_index("ind")
    mine = lax.axis_index("snp")
    bits = [lax.rem(me // (1 << b), 2) for b in range(3)]
    pair = [me + (1 - 2 * bits[b]) * (1 << b) for b in range(3)]
    top = me // 8
    low = lax.rem(me, 8)

    def up(d):
        return lax.rem(top + d, n)

    def side(d):
        return lax.rem(mine + d, n)

    barrier = pltpu.get_barrier_semaphore()
    for b in range(3):
        pl.semaphore_signal(barrier, inc=1, device_id={"ind": pair[b]}, device_id_type=MESH)
    for d in range(1, n):
        pl.semaphore_signal(
            barrier, inc=1, device_id={"ind": low + 8 * up(d)}, device_id_type=MESH
        )
        pl.semaphore_signal(barrier, inc=1, device_id={"snp": side(d)}, device_id_type=MESH)
    pl.semaphore_wait(barrier, 3 + 2 * (n - 1))

    started = []

    def send(src, dst, ssem, rsem, target):
        copy = pltpu.make_async_remote_copy(
            src_ref=src, dst_ref=dst, send_sem=ssem, recv_sem=rsem,
            device_id=target, device_id_type=MESH,
        )
        copy.start()
        started.append(copy)
        return copy

    chunks = [(k, q) for k in range(1, n) for q in range(per)] + [None]
    chunks += [(0, q) for q in range(per)]
    total = len(chunks)
    first, second, third, last, across = {}, {}, {}, {}, {}

    def cols(c):
        k, q = chunks[c]
        return pl.ds((k * per + q) * LANES, LANES)

    def stage0(c):
        if chunks[c] is None:
            src, dst = xpart.at[:, :, 1 - bits[0]], xr0
        else:
            src, dst = part.at[:, :, 1 - bits[0], :, cols(c)], r0.at[c]
        first[c] = send(src, dst, send0.at[c], recv0.at[c], {"ind": pair[0]})

    def stage1(c):
        first[c].wait_recv()
        if chunks[c] is None:
            xh0[...] = xpart[:, :, bits[0]] + xr0[...]
            src, dst = xh0.at[:, 1 - bits[1]], xr1
        else:
            h0[c] = part[:, :, bits[0], :, cols(c)] + r0[c]
            src, dst = h0.at[c, :, 1 - bits[1]], r1.at[c]
        second[c] = send(src, dst, send1.at[c], recv1.at[c], {"ind": pair[1]})

    def stage2(c):
        second[c].wait_recv()
        if chunks[c] is None:
            xyb[mine] = xh0[:, bits[1]] + xr1[...]
            across[c] = [
                send(xyb.at[mine], xyb.at[mine], sendy.at[c, d - 1], recvy.at[c, d - 1], {"snp": side(d)})
                for d in range(1, n)
            ]
        else:
            k, q = chunks[c]
            value = h0[c, :, bits[1]] + r1[c]
            if k == 0:
                yb[q, mine] = value
            else:
                h1[c] = value
                across[k, q] = send(
                    h1.at[c], yb.at[q, mine], sendy.at[c, 0], recvy.at[c, 0], {"snp": side(k)}
                )

    def stage3(c):
        if chunks[c] is None:
            for copy in across[c]:
                copy.wait_recv()
            third[c] = send(
                xyb.at[:, 1 - bits[2]], xr2, send2.at[c], recv2.at[c], {"ind": pair[2]}
            )
        elif chunks[c][0] == 0:
            q = chunks[c][1]
            for k in range(1, n):
                across[k, q].wait_recv()
            third[c] = send(
                yb.at[q, :, 1 - bits[2]], r2.at[q], send2.at[c], recv2.at[c], {"ind": pair[2]}
            )

    def stage4(c):
        if chunks[c] is None:
            third[c].wait_recv()
            xh2[...] = xyb[:, bits[2]] + xr2[...]
            last[c] = [
                send(xh2.at[up(d)], xrf.at[d - 1], sendf.at[c, d - 1], recvf.at[c, d - 1], {"ind": low + 8 * up(d)})
                for d in range(1, n)
            ]
        elif chunks[c][0] == 0:
            q = chunks[c][1]
            third[c].wait_recv()
            h2[q] = yb[q, :, bits[2]] + r2[q]
            last[c] = [
                send(h2.at[q, up(d)], rf.at[q, d - 1], sendf.at[c, d - 1], recvf.at[c, d - 1], {"ind": low + 8 * up(d)})
                for d in range(1, n)
            ]

    def stage5(c):
        if chunks[c] is None:
            value = xh2[top]
            for d in range(1, n):
                last[c][d - 1].wait_recv()
                value = value + xrf[d - 1]
            solved.append(value)
        elif chunks[c][0] == 0:
            q = chunks[c][1]
            value = h2[q, top]
            for d in range(1, n):
                last[c][d - 1].wait_recv()
                value = value + rf[q, d - 1]
            tiles[q] = value

    tiny = {}

    def small_step(b):
        if b > 0:
            tiny[b - 1].wait_recv()
            sbuf[b - 1] = (small[...] if b == 1 else sbuf[b - 2]) + srecv[b - 1]
        if b < 3:
            src = small if b == 0 else sbuf.at[b - 1]
            tiny[b] = send(src, srecv.at[b], ssend.at[b], srec.at[b], {"ind": pair[b]})
        else:
            tiny[3] = [
                send(sbuf.at[2], sfin.at[d - 1], ssend.at[2 + d], srec.at[2 + d], {"ind": low + 8 * up(d)})
                for d in range(1, n)
            ]

    def small_end():
        value = sbuf[2]
        for d in range(1, n):
            tiny[3][d - 1].wait_recv()
            value = value + sfin[d - 1]
        return value

    def start_solve(value):
        rest = value[:k_cov]
        spot = lax.broadcasted_iota(jnp.int32, (k_cov, LANES), 1)
        line = lax.broadcasted_iota(jnp.int32, (k_cov, LANES), 0)
        unit = jnp.where(spot == line, 1.0, 0.0).astype(jnp.float32)
        return jnp.concatenate([rest, unit], axis=1)

    def solve_step(table, step):
        at = per * LANES + step
        row = table[step : step + 1] * lax.rsqrt(table[step : step + 1, at : at + 1])
        factor = table[:, at : at + 1] * lax.rsqrt(table[step : step + 1, at : at + 1])
        line = lax.broadcasted_iota(jnp.int32, table.shape, 0)
        return jnp.where(
            line == step, jnp.broadcast_to(row, table.shape),
            jnp.where(line > step, table - factor * row, table),
        )

    solved, tiles = [], {}
    small_step(0)
    for c in range(total):
        stage0(c)
    stages = [stage1, stage2, stage3, stage4, stage5]
    for tick in range(total + len(stages) - 1):
        for index in range(len(stages)):
            c = tick - index
            if 0 <= c < total:
                stages[index](c)
        if tick < 3:
            small_step(tick + 1)
        if tick == 3:
            sums = small_end()
            table = start_solve(sums)
        if 3 <= tick < 7:
            for step in range((tick - 3) * k_cov // 4, (tick - 2) * k_cov // 4):
                table = solve_step(table, step)

    highest = lax.Precision.HIGHEST
    f32 = jnp.float32
    m = per * LANES
    geno_w = table[:, :m]
    inverse = table[:, m + LANES :]
    variance = sums[k_cov : k_cov + 1, :m] - jnp.sum(geno_w * geno_w, axis=0, keepdims=True)
    packed = solved[0]
    cross = jnp.concatenate(
        [packed] + [pltpu.roll(packed, LANES - g * (k_cov + 1), 1) for g in (1, 2)], axis=0
    )
    trait_w = lax.dot_general(
        cross, inverse, (((1,), (1,)), ((), ())), precision=highest, preferred_element_type=f32
    )
    norm = cross[:, k_cov : k_cov + 1] - jnp.sum(trait_w * trait_w, axis=1, keepdims=True)
    scale = lax.rsqrt(norm / dof + EPS)
    fit = jnp.dot(trait_w, geno_w, precision=highest, preferred_element_type=f32)
    spread = lax.rsqrt(variance + EPS)
    for q in range(per):
        at = slice(q * LANES, (q + 1) * LANES)
        out[:, at] = (tiles[q] - fit[:, at]) * scale * spread[:, at]
    for copy in started:
        copy.wait_send()


def reduce_all(n, k_cov, dof, part, xpart, small):
    rows, width = part.shape[3], part.shape[4]
    per = width // n // LANES
    total = n * per + 1
    xrows = xpart.shape[3]
    f32 = jnp.float32
    dma = pltpu.SemaphoreType.DMA
    vmem = pl.BlockSpec(memory_space=pltpu.VMEM)
    peers = max(n - 1, 1)
    return pl.pallas_call(
        functools.partial(sum_kernel, n, per, k_cov, dof),
        out_shape=jax.ShapeDtypeStruct((rows, per * LANES), f32),
        in_specs=[vmem] * 3,
        out_specs=vmem,
        scratch_shapes=[
            pltpu.VMEM((total, 2, 2, rows, LANES), f32),
            pltpu.VMEM((total, 2, 2, rows, LANES), f32),
            pltpu.VMEM((total, 2, rows, LANES), f32),
            pltpu.VMEM((total, 2, rows, LANES), f32),
            pltpu.VMEM((per, n, 2, rows, LANES), f32),
            pltpu.VMEM((per, n, rows, LANES), f32),
            pltpu.VMEM((per, n, rows, LANES), f32),
            pltpu.VMEM((per, peers, rows, LANES), f32),
            pltpu.VMEM((2, 2, xrows, LANES), f32),
            pltpu.VMEM((2, 2, xrows, LANES), f32),
            pltpu.VMEM((2, xrows, LANES), f32),
            pltpu.VMEM((2, xrows, LANES), f32),
            pltpu.VMEM((n, 2, xrows, LANES), f32),
            pltpu.VMEM((n, xrows, LANES), f32),
            pltpu.VMEM((n, xrows, LANES), f32),
            pltpu.VMEM((peers, xrows, LANES), f32),
            pltpu.VMEM((3,) + small.shape, f32),
            pltpu.VMEM((3,) + small.shape, f32),
            pltpu.VMEM((peers,) + small.shape, f32),
            dma((total,)), dma((total,)), dma((total,)), dma((total,)),
            dma((total, peers)), dma((total, peers)),
            dma((total,)), dma((total,)),
            dma((total, peers)), dma((total, peers)),
            dma((3 + peers,)), dma((3 + peers,)),
        ],
        compiler_params=pltpu.CompilerParams(
            collective_id=0, has_side_effects=True, vmem_limit_bytes=40 << 20
        ),
    )(part, xpart, small)


def per_device(genotypes, covariates, traits):
    n_ind, n_snp = lax.axis_size("ind"), lax.axis_size("snp")
    count = genotypes.shape[0] * n_ind
    k = covariates.shape[1]
    m = genotypes.shape[1]
    width = traits.shape[1]
    block = width // 8
    third = block // 3
    assert n_ind == 8 * n_snp and block % 24 == 0 and m % LANES == 0 and k <= 41
    geno = genotypes.astype(jnp.bfloat16)
    shifted = [geno] + [
        lax.ppermute(geno, "snp", [((s + d) % n_snp, s) for s in range(n_snp)])
        for d in range(1, n_snp)
    ]
    rows = (((0,), (0,)), ((), ()))
    cov = jnp.concatenate(split3(covariates), axis=1)

    gram = lax.dot_general(
        cov, jnp.concatenate([geno, cov], axis=1), rows, preferred_element_type=jnp.float32
    )
    gram = gram[:k] + gram[k : 2 * k] + gram[2 * k :]
    gram_cov = gram[:, m : m + k] + gram[:, m + k : m + 2 * k] + gram[:, m + 2 * k :]
    wide = genotypes.astype(jnp.float32)
    squares = jnp.sum(wide * wide, axis=0)
    small = jnp.concatenate([gram[:, :m], squares[None]], axis=0)
    small = jnp.concatenate([small, jnp.pad(gram_cov, ((0, 1), (0, LANES - k)))], axis=1)
    small = jnp.pad(small, ((0, 7 - k % 8), (0, 0)))

    local = traits.astype(jnp.float32)
    xt = lax.dot_general(traits, cov, rows, preferred_element_type=jnp.float32)
    xt = xt[:, :k] + xt[:, k : 2 * k] + xt[:, 2 * k :]
    xt = jnp.concatenate([xt, jnp.sum(local * local, axis=0)[:, None]], axis=1)
    xt = xt.reshape(8, 3, third, k + 1).transpose(0, 2, 1, 3).reshape(8, third, 3 * (k + 1))
    xt = jnp.pad(xt, ((0, 0), (0, 0), (0, LANES - 3 * (k + 1)))).reshape(2, 2, 2, third, LANES)

    both = jnp.concatenate(shifted, axis=1)
    prod = lax.dot_general(traits, both, rows, preferred_element_type=jnp.float32)
    prod = prod.reshape(2, 2, 2, block, n_snp * m)

    return reduce_all(n_snp, k, count - k, prod, xt, small).T


def solution(mesh):
    in_specs = (P("ind", "snp"), P("ind", None), P("ind", "snp"))
    out_specs = P("snp", "ind")
    return jax.shard_map(
        per_device, mesh=mesh, in_specs=in_specs, out_specs=out_specs, check_vma=False
    )
```

```python
import functools

import jax
import jax.numpy as jnp
from jax import lax
from jax.experimental import pallas as pl
from jax.experimental.pallas import tpu as pltpu
from jax.sharding import PartitionSpec as P

EPS = 1e-05
MESH = pl.DeviceIdType.MESH
LANES = 128


def sum_kernel(
    n, per, k_cov, dof, geno, cov, traits, out,
    tbuf, tt, gown, gother, part, xpart, small, tsem, gsend, grecv,
    r0, h0, r1, h1, yb, r2, h2, rf,
    xr0, xh0, xr1, xh1, xyb, xr2, xh2, xrf,
    sbuf, srecv, sfin,
    send0, recv0, send1, recv1, sendy, recvy, send2, recv2, sendf, recvf, ssend, srec,
):
    me = lax.axis_index("ind")
    mine = lax.axis_index("snp")
    bits = [lax.rem(me // (1 << b), 2) for b in range(3)]
    pair = [me + (1 - 2 * bits[b]) * (1 << b) for b in range(3)]
    top = me // 8
    low = lax.rem(me, 8)

    def up(d):
        return lax.rem(top + d, n)

    def side(d):
        return lax.rem(mine + d, n)

    barrier = pltpu.get_barrier_semaphore()
    for b in range(3):
        pl.semaphore_signal(barrier, inc=1, device_id={"ind": pair[b]}, device_id_type=MESH)
    for d in range(1, n):
        pl.semaphore_signal(
            barrier, inc=1, device_id={"ind": low + 8 * up(d)}, device_id_type=MESH
        )
        pl.semaphore_signal(barrier, inc=1, device_id={"snp": side(d)}, device_id_type=MESH)
    load = pltpu.make_async_copy(traits, tbuf, tsem)
    load.start()

    f32, bf16 = jnp.float32, jnp.bfloat16
    m = per * LANES
    dots = geno[...].astype(f32)
    gown[...] = dots.astype(bf16)
    squares = jnp.sum(dots * dots, axis=0, keepdims=True)
    pl.semaphore_wait(barrier, 3 + 2 * (n - 1))

    started = []

    def send(src, dst, ssem, rsem, target):
        copy = pltpu.make_async_remote_copy(
            src_ref=src, dst_ref=dst, send_sem=ssem, recv_sem=rsem,
            device_id=target, device_id_type=MESH,
        )
        copy.start()
        started.append(copy)
        return copy

    chunks = [None] + [(k, q) for k in range(n) for q in range(per)]
    total = len(chunks)
    first, second, third, last, across = {}, {}, {}, {}, {}

    def cols(c):
        k, q = chunks[c]
        return pl.ds((k * per + q) * LANES, LANES)

    def stage0(c):
        if chunks[c] is None:
            src, dst = xpart.at[:, :, 1 - bits[0]], xr0
        else:
            src, dst = part.at[:, :, 1 - bits[0], :, cols(c)], r0.at[c]
        first[c] = send(src, dst, send0.at[c], recv0.at[c], {"ind": pair[0]})

    def stage1(c):
        first[c].wait_recv()
        if chunks[c] is None:
            xh0[...] = xpart[:, :, bits[0]] + xr0[...]
            src, dst = xh0.at[:, 1 - bits[1]], xr1
        else:
            h0[c] = part[:, :, bits[0], :, cols(c)] + r0[c]
            src, dst = h0.at[c, :, 1 - bits[1]], r1.at[c]
        second[c] = send(src, dst, send1.at[c], recv1.at[c], {"ind": pair[1]})

    def stage2(c):
        second[c].wait_recv()
        if chunks[c] is None:
            xyb[mine] = xh0[:, bits[1]] + xr1[...]
            across[c] = [
                send(xyb.at[mine], xyb.at[mine], sendy.at[c, d - 1], recvy.at[c, d - 1], {"snp": side(d)})
                for d in range(1, n)
            ]
        else:
            k, q = chunks[c]
            value = h0[c, :, bits[1]] + r1[c]
            if k == 0:
                yb[q, mine] = value
            else:
                h1[c] = value
                across[k, q] = send(
                    h1.at[c], yb.at[q, mine], sendy.at[c, 0], recvy.at[c, 0], {"snp": side(k)}
                )

    def stage3(c):
        if chunks[c] is None:
            for copy in across[c]:
                copy.wait_recv()
            third[c] = send(
                xyb.at[:, 1 - bits[2]], xr2, send2.at[c], recv2.at[c], {"ind": pair[2]}
            )
        elif chunks[c][0] == n - 1:
            q = chunks[c][1]
            for k in range(1, n):
                across[k, q].wait_recv()
            third[c] = send(
                yb.at[q, :, 1 - bits[2]], r2.at[q], send2.at[c], recv2.at[c], {"ind": pair[2]}
            )

    def stage4(c):
        if chunks[c] is None:
            third[c].wait_recv()
            xh2[...] = xyb[:, bits[2]] + xr2[...]
            last[c] = [
                send(xh2.at[up(d)], xrf.at[d - 1], sendf.at[c, d - 1], recvf.at[c, d - 1], {"ind": low + 8 * up(d)})
                for d in range(1, n)
            ]
        elif chunks[c][0] == n - 1:
            q = chunks[c][1]
            third[c].wait_recv()
            h2[q] = yb[q, :, bits[2]] + r2[q]
            last[c] = [
                send(h2.at[q, up(d)], rf.at[q, d - 1], sendf.at[c, d - 1], recvf.at[c, d - 1], {"ind": low + 8 * up(d)})
                for d in range(1, n)
            ]

    def stage5(c):
        if chunks[c] is None:
            value = xh2[top]
            for d in range(1, n):
                last[c][d - 1].wait_recv()
                value = value + xrf[d - 1]
            solved.append(value)
        elif chunks[c][0] == n - 1:
            q = chunks[c][1]
            value = h2[q, top]
            for d in range(1, n):
                last[c][d - 1].wait_recv()
                value = value + rf[q, d - 1]
            tiles[q] = value

    tiny = {}

    def small_step(b):
        if b > 0:
            tiny[b - 1].wait_recv()
            sbuf[b - 1] = (small[...] if b == 1 else sbuf[b - 2]) + srecv[b - 1]
        if b < 3:
            src = small if b == 0 else sbuf.at[b - 1]
            tiny[b] = send(src, srecv.at[b], ssend.at[b], srec.at[b], {"ind": pair[b]})
        else:
            tiny[3] = [
                send(sbuf.at[2], sfin.at[d - 1], ssend.at[2 + d], srec.at[2 + d], {"ind": low + 8 * up(d)})
                for d in range(1, n)
            ]

    def small_end():
        value = sbuf[2]
        for d in range(1, n):
            tiny[3][d - 1].wait_recv()
            value = value + sfin[d - 1]
        return value

    def start_solve(value):
        rest = value[:k_cov]
        spot = lax.broadcasted_iota(jnp.int32, (k_cov, LANES), 1)
        line = lax.broadcasted_iota(jnp.int32, (k_cov, LANES), 0)
        unit = jnp.where(spot == line, 1.0, 0.0).astype(jnp.float32)
        return jnp.concatenate([rest, unit], axis=1)

    def solve_step(table, step):
        at = per * LANES + step
        row = table[step : step + 1] * lax.rsqrt(table[step : step + 1, at : at + 1])
        factor = table[:, at : at + 1] * lax.rsqrt(table[step : step + 1, at : at + 1])
        line = lax.broadcasted_iota(jnp.int32, table.shape, 0)
        return jnp.where(
            line == step, jnp.broadcast_to(row, table.shape),
            jnp.where(line > step, table - factor * row, table),
        )

    genos = [
        send(gown, gother.at[d - 1], gsend.at[d - 1], grecv.at[d - 1], {"snp": side(n - d)})
        for d in range(1, n)
    ]

    def fold(x, axis):
        if axis == 0:
            return x[:k_cov] + x[k_cov : 2 * k_cov] + x[2 * k_cov : 3 * k_cov]
        return x + pltpu.roll(x, LANES - k_cov, 1) + pltpu.roll(x, LANES - 2 * k_cov, 1)

    value = cov[...]
    value = jnp.concatenate(
        [value, jnp.zeros((value.shape[0], LANES - k_cov), f32)], axis=1
    )
    high = value.astype(bf16).astype(f32)
    middle = (value - high).astype(bf16).astype(f32)
    low_part = (value - high) - middle
    three = (high + pltpu.roll(middle, k_cov, 1) + pltpu.roll(low_part, 2 * k_cov, 1)).astype(bf16)
    turned = three.T
    gram_g = jnp.dot(turned, gown[...], preferred_element_type=f32)
    gram_c = jnp.dot(turned, three, preferred_element_type=f32)
    small[:k_cov, :m] = fold(gram_g, 0)
    small[:k_cov, m:] = fold(fold(gram_c, 0), 1)
    small[k_cov:, :] = jnp.zeros((small.shape[0] - k_cov, small.shape[1]), f32)
    small[k_cov : k_cov + 1, :m] = squares
    solved, tiles = [], {}
    small_step(0)

    load.wait()

    def turn(t, carry):
        at = pl.ds(pl.multiple_of(t * LANES, LANES), LANES)
        tt[at, :] = tbuf[:, at].T
        return carry

    lax.fori_loop(0, tt.shape[0] // LANES, turn, 0)

    rows = part.shape[3]
    third_rows = rows // 3

    def own(j, carry):
        mat = tt[pl.ds(pl.multiple_of(j * rows, 16), rows), :]
        a, b, c = j // 4, lax.rem(j // 2, 2), lax.rem(j, 2)
        part[a, b, c, :, :m] = jnp.dot(mat, gown[...], preferred_element_type=f32)
        x = fold(jnp.dot(mat, three, preferred_element_type=f32), 1)
        wide = mat.astype(f32)
        norm = jnp.sum(wide * wide, axis=1, keepdims=True)
        lane = lax.broadcasted_iota(jnp.int32, x.shape, 1)
        x = jnp.where(lane < k_cov, x, jnp.where(lane == k_cov, norm, 0.0))
        xpart[a, b, c] = (
            x[:third_rows]
            + pltpu.roll(x[third_rows : 2 * third_rows], k_cov + 1, 1)
            + pltpu.roll(x[2 * third_rows :], 2 * (k_cov + 1), 1)
        )
        return carry

    lax.fori_loop(0, 8, own, 0)
    for c in range(1 + per):
        stage0(c)
    small_step(1)
    stage1(0)
    small_step(2)
    for c in range(1, 1 + per):
        stage1(c)
    small_step(3)
    for k in range(1, n):
        genos[k - 1].wait_recv()

        def other(j, carry, k=k):
            mat = tt[pl.ds(pl.multiple_of(j * rows, 16), rows), :]
            a, b, c = j // 4, lax.rem(j // 2, 2), lax.rem(j, 2)
            part[a, b, c, :, k * m : (k + 1) * m] = jnp.dot(
                mat, gother[k - 1], preferred_element_type=f32
            )
            return carry

        lax.fori_loop(0, 8, other, 0)
        for q in range(per):
            stage0(1 + k * per + q)
    sums = small_end()
    table = start_solve(sums)
    for c in range(1 + per):
        stage2(c)
    late = list(range(1 + per, total))
    stages = [stage1, stage2, stage3, stage4, stage5]
    for tick in range(max(len(late) + len(stages) - 1, 4)):
        for index in range(len(stages)):
            if 0 <= tick - index < len(late):
                stages[index](late[tick - index])
        if tick < 3:
            stages[2 + tick](0)
        if tick < 4:
            for step in range(tick * k_cov // 4, (tick + 1) * k_cov // 4):
                table = solve_step(table, step)

    highest = lax.Precision.HIGHEST
    geno_w = table[:, :m]
    inverse = table[:, m + LANES :]
    variance = sums[k_cov : k_cov + 1, :m] - jnp.sum(geno_w * geno_w, axis=0, keepdims=True)
    packed = solved[0]
    cross = jnp.concatenate(
        [packed] + [pltpu.roll(packed, LANES - g * (k_cov + 1), 1) for g in (1, 2)], axis=0
    )
    trait_w = lax.dot_general(
        cross, inverse, (((1,), (1,)), ((), ())), precision=highest, preferred_element_type=f32
    )
    norm = cross[:, k_cov : k_cov + 1] - jnp.sum(trait_w * trait_w, axis=1, keepdims=True)
    scale = lax.rsqrt(norm / dof + EPS)
    fit = jnp.dot(trait_w, geno_w, precision=highest, preferred_element_type=f32)
    spread = lax.rsqrt(variance + EPS)
    for q in range(per):
        at = slice(q * LANES, (q + 1) * LANES)
        out[:, at] = (tiles[q] - fit[:, at]) * scale * spread[:, at]
    for copy in started:
        copy.wait_send()


def run(n, dof, geno, cov, traits):
    depth, m = geno.shape
    k_cov = cov.shape[1]
    width = traits.shape[1]
    rows = width // 8
    per = m // LANES
    total = n * per + 1
    xrows = rows // 3
    small = jax.ShapeDtypeStruct(((k_cov + 8) // 8 * 8, m + LANES), jnp.float32)
    f32 = jnp.float32
    dma = pltpu.SemaphoreType.DMA
    vmem = pl.BlockSpec(memory_space=pltpu.VMEM)
    peers = max(n - 1, 1)
    return pl.pallas_call(
        functools.partial(sum_kernel, n, per, k_cov, dof),
        out_shape=jax.ShapeDtypeStruct((rows, per * LANES), f32),
        in_specs=[vmem, vmem, pl.BlockSpec(memory_space=pl.ANY)],
        out_specs=vmem,
        scratch_shapes=[
            pltpu.VMEM((depth, width), jnp.bfloat16),
            pltpu.VMEM((width, depth), jnp.bfloat16),
            pltpu.VMEM((depth, m), jnp.bfloat16),
            pltpu.VMEM((peers, depth, m), jnp.bfloat16),
            pltpu.VMEM((2, 2, 2, rows, n * m), f32),
            pltpu.VMEM((2, 2, 2, xrows, LANES), f32),
            pltpu.VMEM(small.shape, f32),
            dma, dma((peers,)), dma((peers,)),
            pltpu.VMEM((total, 2, 2, rows, LANES), f32),
            pltpu.VMEM((total, 2, 2, rows, LANES), f32),
            pltpu.VMEM((total, 2, rows, LANES), f32),
            pltpu.VMEM((total, 2, rows, LANES), f32),
            pltpu.VMEM((per, n, 2, rows, LANES), f32),
            pltpu.VMEM((per, n, rows, LANES), f32),
            pltpu.VMEM((per, n, rows, LANES), f32),
            pltpu.VMEM((per, peers, rows, LANES), f32),
            pltpu.VMEM((2, 2, xrows, LANES), f32),
            pltpu.VMEM((2, 2, xrows, LANES), f32),
            pltpu.VMEM((2, xrows, LANES), f32),
            pltpu.VMEM((2, xrows, LANES), f32),
            pltpu.VMEM((n, 2, xrows, LANES), f32),
            pltpu.VMEM((n, xrows, LANES), f32),
            pltpu.VMEM((n, xrows, LANES), f32),
            pltpu.VMEM((peers, xrows, LANES), f32),
            pltpu.VMEM((3,) + small.shape, f32),
            pltpu.VMEM((3,) + small.shape, f32),
            pltpu.VMEM((peers,) + small.shape, f32),
            dma((total,)), dma((total,)), dma((total,)), dma((total,)),
            dma((total, peers)), dma((total, peers)),
            dma((total,)), dma((total,)),
            dma((total, peers)), dma((total, peers)),
            dma((3 + peers,)), dma((3 + peers,)),
        ],
        compiler_params=pltpu.CompilerParams(
            collective_id=0, has_side_effects=True, vmem_limit_bytes=52 << 20
        ),
    )(geno, cov, traits)


def per_device(genotypes, covariates, traits):
    n_ind, n_snp = lax.axis_size("ind"), lax.axis_size("snp")
    count = genotypes.shape[0] * n_ind
    k = covariates.shape[1]
    assert n_ind == 8 * n_snp and traits.shape[1] % 384 == 0
    assert genotypes.shape[1] % LANES == 0 and k <= 40 and k % 8 == 0
    return run(n_snp, count - k, genotypes, covariates, traits).T


def solution(mesh):
    in_specs = (P("ind", "snp"), P("ind", None), P("ind", "snp"))
    out_specs = P("snp", "ind")
    return jax.shard_map(
        per_device, mesh=mesh, in_specs=in_specs, out_specs=out_specs, check_vma=False
    )
```

```python
import functools

import jax
import jax.numpy as jnp
from jax import lax
from jax.experimental import pallas as pl
from jax.experimental.pallas import tpu as pltpu
from jax.sharding import PartitionSpec as P

EPS = 1e-05
MESH = pl.DeviceIdType.MESH
LANES = 128


def sum_kernel(
    n, per, k_cov, dof, geno, cov, traits, out,
    gbuf, cbuf, tbuf, tt, gown, gother, part, xpart, small, tsem, gsend, grecv,
    r0, h0, r1, h1, r2, h2, yb, rf,
    xr0, xh0, xr1, xh1, xr2, xyb, xrf,
    sbuf, srecv, sfin,
    send0, recv0, send1, recv1, sendy, recvy, send2, recv2, sendf, recvf, ssend, srec,
):
    me = lax.axis_index("ind")
    mine = lax.axis_index("snp")
    bits = [lax.rem(me // (1 << b), 2) for b in range(3)]
    pair = [me + (1 - 2 * bits[b]) * (1 << b) for b in range(3)]
    top = me // 8
    low = lax.rem(me, 8)

    def up(d):
        return lax.rem(top + d, n)

    def side(d):
        return lax.rem(mine + d, n)

    barrier = pltpu.get_barrier_semaphore()
    for b in range(3):
        pl.semaphore_signal(barrier, inc=1, device_id={"ind": pair[b]}, device_id_type=MESH)
    for d in range(1, n):
        pl.semaphore_signal(
            barrier, inc=1, device_id={"ind": low + 8 * up(d)}, device_id_type=MESH
        )
        pl.semaphore_signal(barrier, inc=1, device_id={"snp": side(d)}, device_id_type=MESH)
    loads = [
        pltpu.make_async_copy(src, dst, tsem.at[i])
        for i, (src, dst) in enumerate([(geno, gbuf), (cov, cbuf), (traits, tbuf)])
    ]
    for load in loads:
        load.start()

    f32, bf16 = jnp.float32, jnp.bfloat16
    m = per * LANES
    loads[0].wait()
    dots = gbuf[...].astype(f32)
    gown[...] = dots.astype(bf16)
    squares = jnp.sum(dots * dots, axis=0, keepdims=True)
    pl.semaphore_wait(barrier, 3 + 2 * (n - 1))

    started = []

    def send(src, dst, ssem, rsem, target):
        copy = pltpu.make_async_remote_copy(
            src_ref=src, dst_ref=dst, send_sem=ssem, recv_sem=rsem,
            device_id=target, device_id_type=MESH,
        )
        copy.start()
        started.append(copy)
        return copy

    chunks = [None] + [(k, q) for k in range(n) for q in range(per)]
    total = len(chunks)
    first, second, third, last, across = {}, {}, {}, {}, {}

    def cols(c):
        k, q = chunks[c]
        return pl.ds((k * per + q) * LANES, LANES)

    def stage0(c):
        if chunks[c] is None:
            src, dst = xpart.at[:, :, 1 - bits[0]], xr0
        else:
            src, dst = part.at[:, :, 1 - bits[0], :, cols(c)], r0.at[c]
        first[c] = send(src, dst, send0.at[c], recv0.at[c], {"ind": pair[0]})

    def x_first(c):
        return chunks[c] is not None and chunks[c][1] % 2 == 0

    def stage1(c):
        first[c].wait_recv()
        if chunks[c] is None:
            xh0[...] = xpart[:, :, bits[0]] + xr0[...]
            held, dst = xh0, xr1
        else:
            h0[c] = part[:, :, bits[0], :, cols(c)] + r0[c]
            held, dst = h0.at[c], r1.at[c]
        if x_first(c):
            src, target = held.at[:, 1 - bits[1]], pair[1]
        else:
            src, target = held.at[1 - bits[2]], pair[2]
        second[c] = send(src, dst, send1.at[c], recv1.at[c], {"ind": target})

    def stage2(c):
        second[c].wait_recv()
        bit = 2 if x_first(c) else 1
        if chunks[c] is None:
            xh1[...] = xh0[bits[2]] + xr1[...]
            held, dst = xh1, xr2
        else:
            h1[c] = (h0[c, :, bits[1]] if x_first(c) else h0[c, bits[2]]) + r1[c]
            held, dst = h1.at[c], r2.at[c]
        third[c] = send(
            held.at[1 - bits[bit]], dst, send2.at[c], recv2.at[c], {"ind": pair[bit]}
        )

    def stage3(c):
        third[c].wait_recv()
        bit = 2 if x_first(c) else 1
        if chunks[c] is None:
            xyb[mine] = xh1[bits[bit]] + xr2[...]
            across[c] = [
                send(xyb.at[mine], xyb.at[mine], sendy.at[c, d - 1], recvy.at[c, d - 1], {"snp": side(d)})
                for d in range(1, n)
            ]
        else:
            k, q = chunks[c]
            value = h1[c, bits[bit]] + r2[c]
            if k == 0:
                yb[q, mine] = value
            else:
                h2[c] = value
                across[k, q] = send(
                    h2.at[c], yb.at[q, mine], sendy.at[c, 0], recvy.at[c, 0], {"snp": side(k)}
                )

    def spread_out(c, src, dst):
        last[c] = [
            send(src.at[up(d)], dst.at[d - 1], sendf.at[c, d - 1], recvf.at[c, d - 1], {"ind": low + 8 * up(d)})
            for d in range(1, n)
        ]

    def stage4(c):
        if chunks[c] is None:
            for copy in across[c]:
                copy.wait_recv()
            spread_out(c, xyb, xrf)
        elif chunks[c][0] == n - 1:
            q = chunks[c][1]
            for k in range(1, n):
                across[k, q].wait_recv()
            spread_out(c, yb.at[q], rf.at[q])

    def stage5(c):
        if chunks[c] is None:
            value = xyb[top]
            for d in range(1, n):
                last[c][d - 1].wait_recv()
                value = value + xrf[d - 1]
            solved.append(value)
        elif chunks[c][0] == n - 1:
            q = chunks[c][1]
            value = yb[q, top]
            for d in range(1, n):
                last[c][d - 1].wait_recv()
                value = value + rf[q, d - 1]
            tiles[q] = value

    tiny = {}

    def small_step(b):
        if b > 0:
            tiny[b - 1].wait_recv()
            sbuf[b - 1] = (small[...] if b == 1 else sbuf[b - 2]) + srecv[b - 1]
        if b < 3:
            src = small if b == 0 else sbuf.at[b - 1]
            tiny[b] = send(src, srecv.at[b], ssend.at[b], srec.at[b], {"ind": pair[b]})
        else:
            tiny[3] = [
                send(sbuf.at[2], sfin.at[d - 1], ssend.at[2 + d], srec.at[2 + d], {"ind": low + 8 * up(d)})
                for d in range(1, n)
            ]

    def small_end():
        value = sbuf[2]
        for d in range(1, n):
            tiny[3][d - 1].wait_recv()
            value = value + sfin[d - 1]
        return value

    def start_solve(value):
        rest = value[:k_cov]
        spot = lax.broadcasted_iota(jnp.int32, (k_cov, LANES), 1)
        line = lax.broadcasted_iota(jnp.int32, (k_cov, LANES), 0)
        unit = jnp.where(spot == line, 1.0, 0.0).astype(jnp.float32)
        return jnp.concatenate([rest, unit], axis=1)

    def solve_step(table, step):
        at = per * LANES + step
        row = table[step : step + 1] * lax.rsqrt(table[step : step + 1, at : at + 1])
        factor = table[:, at : at + 1] * lax.rsqrt(table[step : step + 1, at : at + 1])
        line = lax.broadcasted_iota(jnp.int32, table.shape, 0)
        return jnp.where(
            line == step, jnp.broadcast_to(row, table.shape),
            jnp.where(line > step, table - factor * row, table),
        )

    def lanes(q):
        return pl.ds(q * LANES, LANES)

    genos = {}
    for q in range(per):
        for d in range(1, n):
            genos[d, q] = send(
                gown.at[:, lanes(q)], gother.at[d - 1, :, lanes(q)],
                gsend.at[d - 1, q], grecv.at[d - 1, q], {"snp": side(n - d)},
            )

    def fold(x, axis):
        if axis == 0:
            return x[:k_cov] + x[k_cov : 2 * k_cov] + x[2 * k_cov : 3 * k_cov]
        return x + pltpu.roll(x, LANES - k_cov, 1) + pltpu.roll(x, LANES - 2 * k_cov, 1)

    loads[1].wait()
    value = cbuf[...]
    high = value.astype(bf16).astype(f32)
    middle = (value - high).astype(bf16).astype(f32)
    rest = (value - high) - middle
    blank = jnp.zeros((LANES - 3 * k_cov, value.shape[1]), f32)
    turned = jnp.concatenate([high, middle, rest, blank], axis=0).astype(bf16)
    three = turned.T
    gram_g = jnp.dot(turned, gown[...], preferred_element_type=f32)
    gram_c = jnp.dot(turned, three, preferred_element_type=f32)
    small[:k_cov, :m] = fold(gram_g, 0)
    small[:k_cov, m:] = fold(fold(gram_c, 0), 1)
    small[k_cov:, :] = jnp.zeros((small.shape[0] - k_cov, small.shape[1]), f32)
    small[k_cov : k_cov + 1, :m] = squares
    solved, tiles = [], {}
    small_step(0)

    loads[2].wait()

    def turn(t, carry):
        at = pl.ds(pl.multiple_of(t * LANES, LANES), LANES)
        tt[at, :] = tbuf[:, at].T
        return carry

    lax.fori_loop(0, tt.shape[0] // LANES, turn, 0)

    rows = part.shape[3]
    third_rows = rows // 3

    def own(j, carry):
        mat = tt[pl.ds(pl.multiple_of(j * rows, 16), rows), :]
        a, b, c = j // 4, lax.rem(j // 2, 2), lax.rem(j, 2)
        part[a, b, c, :, :m] = jnp.dot(mat, gown[...], preferred_element_type=f32)
        x = fold(jnp.dot(mat, three, preferred_element_type=f32), 1)
        wide = mat.astype(f32)
        norm = jnp.sum(wide * wide, axis=1, keepdims=True)
        lane = lax.broadcasted_iota(jnp.int32, x.shape, 1)
        x = jnp.where(lane < k_cov, x, jnp.where(lane == k_cov, norm, 0.0))
        xpart[a, b, c] = (
            x[:third_rows]
            + pltpu.roll(x[third_rows : 2 * third_rows], k_cov + 1, 1)
            + pltpu.roll(x[2 * third_rows :], 2 * (k_cov + 1), 1)
        )
        return carry

    lax.fori_loop(0, 8, own, 0)
    for c in range(1 + per):
        stage0(c)
    small_step(1)
    stage1(0)
    small_step(2)
    for c in range(1, 1 + per):
        stage1(c)
    small_step(3)
    early = list(range(1 + per))
    for k in range(1, n):
        for q in range(per):
            genos[k, q].wait_recv()

            def other(j, carry, k=k, q=q):
                mat = tt[pl.ds(pl.multiple_of(j * rows, 16), rows), :]
                a, b, c = j // 4, lax.rem(j // 2, 2), lax.rem(j, 2)
                part[a, b, c, :, lanes(k * per + q)] = jnp.dot(
                    mat, gother[k - 1, :, lanes(q)], preferred_element_type=f32
                )
                return carry

            lax.fori_loop(0, 8, other, 0)
            stage0(1 + k * per + q)
            if early:
                stage2(early.pop(0))
    while early:
        stage2(early.pop(0))
    sums = small_end()
    table = start_solve(sums)
    for c in range(1 + per):
        stage3(c)
    late = list(range(1 + per, total))
    stages = [stage1, stage2, stage3, stage4, stage5]
    for tick in range(max(len(late) + len(stages) - 1, 4)):
        for index in range(len(stages)):
            if 0 <= tick - index < len(late):
                stages[index](late[tick - index])
        if tick < 2:
            stages[3 + tick](0)
        if tick < 4:
            for step in range(tick * k_cov // 4, (tick + 1) * k_cov // 4):
                table = solve_step(table, step)

    highest = lax.Precision.HIGHEST
    geno_w = table[:, :m]
    inverse = table[:, m + LANES :]
    variance = sums[k_cov : k_cov + 1, :m] - jnp.sum(geno_w * geno_w, axis=0, keepdims=True)
    packed = solved[0]
    cross = jnp.concatenate(
        [packed] + [pltpu.roll(packed, LANES - g * (k_cov + 1), 1) for g in (1, 2)], axis=0
    )
    trait_w = lax.dot_general(
        cross, inverse, (((1,), (1,)), ((), ())), precision=highest, preferred_element_type=f32
    )
    norm = cross[:, k_cov : k_cov + 1] - jnp.sum(trait_w * trait_w, axis=1, keepdims=True)
    scale = lax.rsqrt(norm / dof + EPS)
    fit = jnp.dot(trait_w, geno_w, precision=highest, preferred_element_type=f32)
    spread = lax.rsqrt(variance + EPS)
    for q in range(per):
        at = slice(q * LANES, (q + 1) * LANES)
        out[:, at] = (tiles[q] - fit[:, at]) * scale * spread[:, at]
    for copy in started:
        copy.wait_send()


def run(n, dof, geno, cov, traits):
    depth, m = geno.shape
    k_cov = cov.shape[0]
    width = traits.shape[1]
    rows = width // 8
    per = m // LANES
    total = n * per + 1
    xrows = rows // 3
    small = jax.ShapeDtypeStruct(((k_cov + 8) // 8 * 8, m + LANES), jnp.float32)
    f32 = jnp.float32
    dma = pltpu.SemaphoreType.DMA
    vmem = pl.BlockSpec(memory_space=pltpu.VMEM)
    peers = max(n - 1, 1)
    return pl.pallas_call(
        functools.partial(sum_kernel, n, per, k_cov, dof),
        out_shape=jax.ShapeDtypeStruct((rows, per * LANES), f32),
        in_specs=[pl.BlockSpec(memory_space=pltpu.HBM)] * 3,
        out_specs=vmem,
        scratch_shapes=[
            pltpu.VMEM((depth, m), jnp.int32),
            pltpu.VMEM((k_cov, depth), f32),
            pltpu.VMEM((depth, width), jnp.bfloat16),
            pltpu.VMEM((width, depth), jnp.bfloat16),
            pltpu.VMEM((depth, m), jnp.bfloat16),
            pltpu.VMEM((peers, depth, m), jnp.bfloat16),
            pltpu.VMEM((2, 2, 2, rows, n * m), f32),
            pltpu.VMEM((2, 2, 2, xrows, LANES), f32),
            pltpu.VMEM(small.shape, f32),
            dma((3,)), dma((peers, per)), dma((peers, per)),
            pltpu.VMEM((total, 2, 2, rows, LANES), f32),
            pltpu.VMEM((total, 2, 2, rows, LANES), f32),
            pltpu.VMEM((total, 2, rows, LANES), f32),
            pltpu.VMEM((total, 2, rows, LANES), f32),
            pltpu.VMEM((total, rows, LANES), f32),
            pltpu.VMEM((total, rows, LANES), f32),
            pltpu.VMEM((per, n, rows, LANES), f32),
            pltpu.VMEM((per, peers, rows, LANES), f32),
            pltpu.VMEM((2, 2, xrows, LANES), f32),
            pltpu.VMEM((2, 2, xrows, LANES), f32),
            pltpu.VMEM((2, xrows, LANES), f32),
            pltpu.VMEM((2, xrows, LANES), f32),
            pltpu.VMEM((xrows, LANES), f32),
            pltpu.VMEM((n, xrows, LANES), f32),
            pltpu.VMEM((peers, xrows, LANES), f32),
            pltpu.VMEM((3,) + small.shape, f32),
            pltpu.VMEM((3,) + small.shape, f32),
            pltpu.VMEM((peers,) + small.shape, f32),
            dma((total,)), dma((total,)), dma((total,)), dma((total,)),
            dma((total, peers)), dma((total, peers)),
            dma((total,)), dma((total,)),
            dma((total, peers)), dma((total, peers)),
            dma((3 + peers,)), dma((3 + peers,)),
        ],
        compiler_params=pltpu.CompilerParams(
            collective_id=0, has_side_effects=True, vmem_limit_bytes=52 << 20
        ),
    )(geno, cov, traits)


def per_device(genotypes, covariates, traits):
    n_ind, n_snp = lax.axis_size("ind"), lax.axis_size("snp")
    count = genotypes.shape[0] * n_ind
    k = covariates.shape[1]
    assert n_ind == 8 * n_snp and traits.shape[1] % 384 == 0
    assert genotypes.shape[1] % LANES == 0 and k <= 40 and k % 8 == 0
    return run(n_snp, count - k, genotypes, covariates.T, traits).T


def solution(mesh):
    in_specs = (P("ind", "snp"), P("ind", None), P("ind", "snp"))
    out_specs = P("snp", "ind")
    return jax.shard_map(
        per_device, mesh=mesh, in_specs=in_specs, out_specs=out_specs, check_vma=False
    )
```

```python
import functools

import jax
import jax.numpy as jnp
from jax import lax
from jax.experimental import pallas as pl
from jax.experimental.pallas import tpu as pltpu
from jax.sharding import PartitionSpec as P

EPS = 1e-05
MESH = pl.DeviceIdType.MESH
LANES = 128


def sum_kernel(
    n, per, k_cov, dof, geno, cov, traits, out,
    gbuf, cbuf, tbuf, tt, gown, gother, part, xpart, small, tsem, gsend, grecv,
    r0, h0, r1, h1, r2, h2, yb, rf,
    xr0, xh0, xr1, xh1, xr2, xyb, xrf,
    sbuf, srecv, sfin,
    send0, recv0, send1, recv1, sendy, recvy, send2, recv2, sendf, recvf, ssend, srec,
):
    me = lax.axis_index("ind")
    mine = lax.axis_index("snp")
    bits = [lax.rem(me // (1 << b), 2) for b in range(3)]
    pair = [me + (1 - 2 * bits[b]) * (1 << b) for b in range(3)]
    top = me // 8
    low = lax.rem(me, 8)

    def up(d):
        return lax.rem(top + d, n)

    def side(d):
        return lax.rem(mine + d, n)

    barrier = pltpu.get_barrier_semaphore()
    for b in range(3):
        pl.semaphore_signal(barrier, inc=1, device_id={"ind": pair[b]}, device_id_type=MESH)
    for d in range(1, n):
        pl.semaphore_signal(
            barrier, inc=1, device_id={"ind": low + 8 * up(d)}, device_id_type=MESH
        )
        pl.semaphore_signal(barrier, inc=1, device_id={"snp": side(d)}, device_id_type=MESH)
    loads = [
        pltpu.make_async_copy(src, dst, tsem.at[i])
        for i, (src, dst) in enumerate([(geno, gbuf), (cov, cbuf), (traits, tbuf)])
    ]
    for load in loads:
        load.start()

    f32, bf16 = jnp.float32, jnp.bfloat16
    m = per * LANES
    loads[0].wait()
    dots = gbuf[...].astype(f32)
    gown[...] = dots.astype(bf16)
    squares = jnp.sum(dots * dots, axis=0, keepdims=True)
    pl.semaphore_wait(barrier, 3 + 2 * (n - 1))

    started = []

    def send(src, dst, ssem, rsem, target):
        copy = pltpu.make_async_remote_copy(
            src_ref=src, dst_ref=dst, send_sem=ssem, recv_sem=rsem,
            device_id=target, device_id_type=MESH,
        )
        copy.start()
        started.append(copy)
        return copy

    chunks = [None] + [(k, q) for k in range(n) for q in range(per)]
    total = len(chunks)
    first, second, third, last, across = {}, {}, {}, {}, {}

    def cols(c):
        k, q = chunks[c]
        return pl.ds((k * per + q) * LANES, LANES)

    def stage0(c):
        if chunks[c] is None:
            src, dst = xpart.at[:, :, 1 - bits[0]], xr0
        else:
            src, dst = part.at[:, :, 1 - bits[0], :, cols(c)], r0.at[c]
        first[c] = send(src, dst, send0.at[c], recv0.at[c], {"ind": pair[0]})

    def x_first(c):
        return chunks[c] is not None and chunks[c][1] % 2 == 0

    def stage1(c):
        first[c].wait_recv()
        if chunks[c] is None:
            xh0[...] = xpart[:, :, bits[0]] + xr0[...]
            held, dst = xh0, xr1
        else:
            h0[c] = part[:, :, bits[0], :, cols(c)] + r0[c]
            held, dst = h0.at[c], r1.at[c]
        if x_first(c):
            src, target = held.at[:, 1 - bits[1]], pair[1]
        else:
            src, target = held.at[1 - bits[2]], pair[2]
        second[c] = send(src, dst, send1.at[c], recv1.at[c], {"ind": target})

    def stage2(c):
        second[c].wait_recv()
        bit = 2 if x_first(c) else 1
        if chunks[c] is None:
            xh1[...] = xh0[bits[2]] + xr1[...]
            held, dst = xh1, xr2
        else:
            h1[c] = (h0[c, :, bits[1]] if x_first(c) else h0[c, bits[2]]) + r1[c]
            held, dst = h1.at[c], r2.at[c]
        third[c] = send(
            held.at[1 - bits[bit]], dst, send2.at[c], recv2.at[c], {"ind": pair[bit]}
        )

    def stage3(c):
        third[c].wait_recv()
        bit = 2 if x_first(c) else 1
        if chunks[c] is None:
            xyb[mine] = xh1[bits[bit]] + xr2[...]
            across[c] = [
                send(xyb.at[mine], xyb.at[mine], sendy.at[c, d - 1], recvy.at[c, d - 1], {"snp": side(d)})
                for d in range(1, n)
            ]
        else:
            k, q = chunks[c]
            value = h1[c, bits[bit]] + r2[c]
            if k == 0:
                yb[q, mine] = value
            else:
                h2[c] = value
                across[k, q] = send(
                    h2.at[c], yb.at[q, mine], sendy.at[c, 0], recvy.at[c, 0], {"snp": side(k)}
                )

    def spread_out(c, src, dst):
        last[c] = [
            send(src.at[up(d)], dst.at[d - 1], sendf.at[c, d - 1], recvf.at[c, d - 1], {"ind": low + 8 * up(d)})
            for d in range(1, n)
        ]

    def stage4(c):
        if chunks[c] is None:
            for copy in across[c]:
                copy.wait_recv()
            spread_out(c, xyb, xrf)
        elif chunks[c][0] == n - 1:
            q = chunks[c][1]
            for k in range(1, n):
                across[k, q].wait_recv()
            spread_out(c, yb.at[q], rf.at[q])

    def stage5(c):
        if chunks[c] is None:
            value = xyb[top]
            for d in range(1, n):
                last[c][d - 1].wait_recv()
                value = value + xrf[d - 1]
            solved.append(value)
        elif chunks[c][0] == n - 1:
            q = chunks[c][1]
            value = yb[q, top]
            for d in range(1, n):
                last[c][d - 1].wait_recv()
                value = value + rf[q, d - 1]
            tiles[q] = value

    tiny = {}

    def small_step(b):
        if b > 0:
            tiny[b - 1].wait_recv()
            sbuf[b - 1] = (small[...] if b == 1 else sbuf[b - 2]) + srecv[b - 1]
        if b < 3:
            src = small if b == 0 else sbuf.at[b - 1]
            tiny[b] = send(src, srecv.at[b], ssend.at[b], srec.at[b], {"ind": pair[b]})
        else:
            tiny[3] = [
                send(sbuf.at[2], sfin.at[d - 1], ssend.at[2 + d], srec.at[2 + d], {"ind": low + 8 * up(d)})
                for d in range(1, n)
            ]

    def small_end():
        value = sbuf[2]
        for d in range(1, n):
            tiny[3][d - 1].wait_recv()
            value = value + sfin[d - 1]
        return value

    def start_solve(value):
        rest = value[:k_cov]
        spot = lax.broadcasted_iota(jnp.int32, (k_cov, LANES), 1)
        line = lax.broadcasted_iota(jnp.int32, (k_cov, LANES), 0)
        unit = jnp.where(spot == line, 1.0, 0.0).astype(jnp.float32)
        return jnp.concatenate([rest, unit], axis=1)

    def solve_step(table, step):
        at = per * LANES + step
        root = lax.rsqrt(table[step : step + 1, at : at + 1])
        row = table[step : step + 1] * root
        factor = table[:, at : at + 1] * root
        line = lax.broadcasted_iota(jnp.int32, table.shape, 0)
        return jnp.where(
            line == step, jnp.broadcast_to(row, table.shape),
            jnp.where(line > step, table - factor * row, table),
        )

    def lanes(q):
        return pl.ds(q * LANES, LANES)

    genos = {}
    for q in range(per):
        for d in range(1, n):
            genos[d, q] = send(
                gown.at[:, lanes(q)], gother.at[d - 1, :, lanes(q)],
                gsend.at[d - 1, q], grecv.at[d - 1, q], {"snp": side(n - d)},
            )

    def fold(x, axis):
        if axis == 0:
            return x[:k_cov] + x[k_cov : 2 * k_cov] + x[2 * k_cov : 3 * k_cov]
        return x + pltpu.roll(x, LANES - k_cov, 1) + pltpu.roll(x, LANES - 2 * k_cov, 1)

    loads[1].wait()
    value = cbuf[...]
    high = value.astype(bf16).astype(f32)
    middle = (value - high).astype(bf16).astype(f32)
    rest = (value - high) - middle
    blank = jnp.zeros((LANES - 3 * k_cov, value.shape[1]), f32)
    turned = jnp.concatenate([high, middle, rest, blank], axis=0).astype(bf16)
    three = turned.T
    gram_g = jnp.dot(turned, gown[...], preferred_element_type=f32)
    gram_c = jnp.dot(turned, three, preferred_element_type=f32)
    small[:k_cov, :m] = fold(gram_g, 0)
    small[:k_cov, m:] = fold(fold(gram_c, 0), 1)
    small[k_cov:, :] = jnp.zeros((small.shape[0] - k_cov, small.shape[1]), f32)
    small[k_cov : k_cov + 1, :m] = squares
    solved, tiles = [], {}
    small_step(0)

    loads[2].wait()

    def turn(t, carry):
        at = pl.ds(pl.multiple_of(t * LANES, LANES), LANES)
        tt[at, :] = tbuf[:, at].T
        return carry

    lax.fori_loop(0, tt.shape[0] // LANES, turn, 0)

    rows = part.shape[3]
    third_rows = rows // 3

    def own(j, carry):
        mat = tt[pl.ds(pl.multiple_of(j * rows, 16), rows), :]
        a, b, c = j // 4, lax.rem(j // 2, 2), lax.rem(j, 2)
        part[a, b, c, :, :m] = jnp.dot(mat, gown[...], preferred_element_type=f32)
        x = fold(jnp.dot(mat, three, preferred_element_type=f32), 1)
        wide = mat.astype(f32)
        norm = jnp.sum(wide * wide, axis=1, keepdims=True)
        lane = lax.broadcasted_iota(jnp.int32, x.shape, 1)
        x = jnp.where(lane < k_cov, x, jnp.where(lane == k_cov, norm, 0.0))
        xpart[a, b, c] = (
            x[:third_rows]
            + pltpu.roll(x[third_rows : 2 * third_rows], k_cov + 1, 1)
            + pltpu.roll(x[2 * third_rows :], 2 * (k_cov + 1), 1)
        )
        return carry

    lax.fori_loop(0, 8, own, 0)
    for c in range(1 + per):
        stage0(c)
    small_step(1)
    stage1(0)
    small_step(2)
    for c in range(1, 1 + per):
        stage1(c)
    small_step(3)
    early = list(range(1 + per))
    for k in range(1, n):
        for q in range(per):
            genos[k, q].wait_recv()

            def other(j, carry, k=k, q=q):
                mat = tt[pl.ds(pl.multiple_of(j * rows, 16), rows), :]
                a, b, c = j // 4, lax.rem(j // 2, 2), lax.rem(j, 2)
                part[a, b, c, :, lanes(k * per + q)] = jnp.dot(
                    mat, gother[k - 1, :, lanes(q)], preferred_element_type=f32
                )
                return carry

            lax.fori_loop(0, 8, other, 0)
            stage0(1 + k * per + q)
            if early:
                stage2(early.pop(0))
    while early:
        stage2(early.pop(0))
    sums = small_end()
    table = start_solve(sums)
    for c in range(1 + per):
        stage3(c)
    late = list(range(1 + per, total))
    stages = [stage1, stage2, stage3, stage4, stage5]
    highest = lax.Precision.HIGHEST
    cut = k_cov * 7 // 10
    for tick in range(len(late) + len(stages) - 1):
        for index in range(len(stages)):
            if index == 1:
                for step in range(cut) if tick == 1 else ():
                    table = solve_step(table, step)
            if index == 2:
                for step in range(cut, k_cov) if tick == 2 else ():
                    table = solve_step(table, step)
            if index == 4 and tick == 4:
                geno_w = table[:, :m]
                inverse = table[:, m + LANES :]
                variance = sums[k_cov : k_cov + 1, :m] - jnp.sum(
                    geno_w * geno_w, axis=0, keepdims=True
                )
                packed = solved[0]
                cross = jnp.concatenate(
                    [packed] + [pltpu.roll(packed, LANES - g * (k_cov + 1), 1) for g in (1, 2)],
                    axis=0,
                )
                trait_w = lax.dot_general(
                    cross, inverse, (((1,), (1,)), ((), ())), precision=highest,
                    preferred_element_type=f32,
                )
                norm = cross[:, k_cov : k_cov + 1] - jnp.sum(
                    trait_w * trait_w, axis=1, keepdims=True
                )
                scale = lax.rsqrt(norm / dof + EPS)
                fit = jnp.dot(trait_w, geno_w, precision=highest, preferred_element_type=f32)
                spread = lax.rsqrt(variance + EPS)
            if 0 <= tick - index < len(late):
                c = late[tick - index]
                stages[index](c)
                if index == 4 and chunks[c][0] == n - 1:
                    q = chunks[c][1]
                    at = slice(q * LANES, (q + 1) * LANES)
                    out[:, at] = (tiles[q] - fit[:, at]) * scale * spread[:, at]
        if tick < 2:
            stages[3 + tick](0)

    for copy in started:
        copy.wait_send()


def run(n, dof, geno, cov, traits):
    depth, m = geno.shape
    k_cov = cov.shape[0]
    width = traits.shape[1]
    rows = width // 8
    per = m // LANES
    total = n * per + 1
    xrows = rows // 3
    small = jax.ShapeDtypeStruct(((k_cov + 8) // 8 * 8, m + LANES), jnp.float32)
    f32 = jnp.float32
    dma = pltpu.SemaphoreType.DMA
    vmem = pl.BlockSpec(memory_space=pltpu.VMEM)
    peers = max(n - 1, 1)
    return pl.pallas_call(
        functools.partial(sum_kernel, n, per, k_cov, dof),
        out_shape=jax.ShapeDtypeStruct((rows, per * LANES), f32),
        in_specs=[pl.BlockSpec(memory_space=pltpu.HBM)] * 3,
        out_specs=vmem,
        scratch_shapes=[
            pltpu.VMEM((depth, m), jnp.int32),
            pltpu.VMEM((k_cov, depth), f32),
            pltpu.VMEM((depth, width), jnp.bfloat16),
            pltpu.VMEM((width, depth), jnp.bfloat16),
            pltpu.VMEM((depth, m), jnp.bfloat16),
            pltpu.VMEM((peers, depth, m), jnp.bfloat16),
            pltpu.VMEM((2, 2, 2, rows, n * m), f32),
            pltpu.VMEM((2, 2, 2, xrows, LANES), f32),
            pltpu.VMEM(small.shape, f32),
            dma((3,)), dma((peers, per)), dma((peers, per)),
            pltpu.VMEM((total, 2, 2, rows, LANES), f32),
            pltpu.VMEM((total, 2, 2, rows, LANES), f32),
            pltpu.VMEM((total, 2, rows, LANES), f32),
            pltpu.VMEM((total, 2, rows, LANES), f32),
            pltpu.VMEM((total, rows, LANES), f32),
            pltpu.VMEM((total, rows, LANES), f32),
            pltpu.VMEM((per, n, rows, LANES), f32),
            pltpu.VMEM((per, peers, rows, LANES), f32),
            pltpu.VMEM((2, 2, xrows, LANES), f32),
            pltpu.VMEM((2, 2, xrows, LANES), f32),
            pltpu.VMEM((2, xrows, LANES), f32),
            pltpu.VMEM((2, xrows, LANES), f32),
            pltpu.VMEM((xrows, LANES), f32),
            pltpu.VMEM((n, xrows, LANES), f32),
            pltpu.VMEM((peers, xrows, LANES), f32),
            pltpu.VMEM((3,) + small.shape, f32),
            pltpu.VMEM((3,) + small.shape, f32),
            pltpu.VMEM((peers,) + small.shape, f32),
            dma((total,)), dma((total,)), dma((total,)), dma((total,)),
            dma((total, peers)), dma((total, peers)),
            dma((total,)), dma((total,)),
            dma((total, peers)), dma((total, peers)),
            dma((3 + peers,)), dma((3 + peers,)),
        ],
        compiler_params=pltpu.CompilerParams(
            collective_id=0, has_side_effects=True, vmem_limit_bytes=62 << 20
        ),
    )(geno, cov, traits)


def per_device(genotypes, covariates, traits):
    n_ind, n_snp = lax.axis_size("ind"), lax.axis_size("snp")
    count = genotypes.shape[0] * n_ind
    k = covariates.shape[1]
    assert n_ind == 8 * n_snp and traits.shape[1] % 384 == 0
    assert genotypes.shape[1] % LANES == 0 and k <= 40 and k % 8 == 0
    return run(n_snp, count - k, genotypes, covariates.T, traits).T


def solution(mesh):
    in_specs = (P("ind", "snp"), P("ind", None), P("ind", "snp"))
    out_specs = P("snp", "ind")
    return jax.shard_map(
        per_device, mesh=mesh, in_specs=in_specs, out_specs=out_specs, check_vma=False
    )
```
